32 devices in a mesh: pair: 8 (over z, y), occ: 4 (over x, core).
Axes of the slice: x: 2, y: 2, z: 4, core: 2. Of those that a mesh axis runs over, the one named last changes fastest.
Arguments:
- half_ints: bfloat16 [2, 896, 4, 896], P(None, 'pair', 'occ'), may hold values from -6 to 6
- coeffs: bfloat16 [896, 768], P('occ'), may hold values from -0.1875 to 0.1875
- pair_map: int32 [8], replicated, may hold values from 0 to 7, each once
- tile_table: int32 [8], replicated, may hold values from 0 to 7, each once
Outputs:
- mo_ints: float32 [1536, 4, 768], P('pair', 'occ')
The draws below stay inside these ranges and needn't reach their ends.
Inputs may be any that keep to these rules, and one draw needn't show every extreme that they name: pair_map is a permutation of 0 to 7. tile_table is a permutation of 0 to 7.
All inputs are finite; a program needn't handle non-finite values.
Results may differ from the reference program's by a relative error of at most 0.0029.
Values may be sent and summed in bfloat16 or wider, within the bound.
A program may use at most 64 MiB of HBM per device.

```python
import jax
import jax.numpy as jnp

NBF = 896
NV = 768
I = 2
J = 4
N_PAIR = 8


def shard_levels(stream_key, dims, shards, smallest, largest):
    factor_of = 1.0
    for dim, parts in shards:
        steps = jax.random.uniform(jax.random.fold_in(jax.random.fold_in(stream_key, 6), dim), (parts,), jnp.float32, smallest / len(shards), largest / len(shards))
        factor_of = factor_of * jnp.repeat(jnp.exp(steps), dims[dim] // parts).reshape((-1,) + (1,) * (len(dims) - 1 - dim))
    return factor_of


def bell_draw(stream_key, extent, deviation, most, cuts=(), kind=jnp.bfloat16):
    entries = jax.random.normal(stream_key, extent, jnp.float32) * deviation
    if len(cuts) > 0:
        entries = shard_levels(stream_key, extent, cuts, -0.22, 0.18) * entries
    return jnp.clip(entries, min=-most, max=most).astype(kind)


def setup_inputs(seed: int = 0) -> dict:
    arg_keys = jax.random.split(jax.random.key(seed), 5)
    return {
        "half_ints": bell_draw(arg_keys[0], (I, NBF, J, NBF), 1.0, 6.0, ((1, 8), (2, 4))),
        "coeffs": bell_draw(arg_keys[1], (NBF, NV), NBF ** -0.5, 0.1875, ((0, 4),)),
        "pair_map": jax.random.permutation(arg_keys[2], N_PAIR).astype(jnp.int32),
        "tile_table": jax.random.permutation(arg_keys[3], N_PAIR).astype(jnp.int32),
    }


def reference(half_ints, coeffs, pair_map, tile_table):
    sblock = NBF // N_PAIR
    tile_rows = I * NV // N_PAIR
    split = half_ints.reshape(I, N_PAIR, sblock, J, NBF)
    natural = jnp.zeros_like(split).at[:, pair_map].set(split).reshape(I, NBF, J, NBF)
    half_mo = jnp.einsum("isjr,rb->isjb", natural.astype(jnp.float32), coeffs.astype(jnp.float32)).astype(jnp.bfloat16)
    full = jnp.einsum("sa,isjb->iajb", coeffs.astype(jnp.float32), half_mo.astype(jnp.float32))
    tiles = full.reshape(N_PAIR, tile_rows, J, NV)[tile_table]
    return tiles.reshape(I * NV, J, NV)
```

```python
import functools

import jax
import jax.numpy as jnp
from jax import lax
from jax.experimental import pallas as pl
from jax.experimental.pallas import tpu as pltpu
from jax.sharding import PartitionSpec as P


def shards_general(half_ints, coeffs, pair_map, tile_table):
    num_occ = half_ints.shape[0]
    sblock = half_ints.shape[1]
    local_j = half_ints.shape[2]
    num_basis = half_ints.shape[3]
    num_virt = coeffs.shape[1]
    num_pair = lax.axis_size("pair")
    tile_rows = num_occ * num_virt // num_pair
    all_coeffs = lax.all_gather(coeffs, "occ", axis=0, tiled=True)
    flat_ints = half_ints.reshape(num_occ * sblock * local_j, num_basis)
    half_mo = jnp.dot(flat_ints, all_coeffs, preferred_element_type=jnp.float32).astype(
        jnp.bfloat16
    )
    half_mo = half_mo.reshape(num_occ, sblock, local_j, num_virt)
    tile_id = tile_table[lax.axis_index("pair")]
    virt_start = tile_id * tile_rows % num_virt
    column_coeffs = lax.dynamic_slice_in_dim(all_coeffs, virt_start, tile_rows, 1)
    half_flat = half_mo.reshape(num_occ, sblock, local_j * num_virt)
    slot_occ = tile_table * tile_rows // num_virt
    outgoing = jnp.take(half_flat, slot_occ, axis=0)
    incoming = lax.all_to_all(outgoing, "pair", split_axis=0, concat_axis=0, tiled=True)
    block_coeffs = jnp.take(column_coeffs.reshape(num_pair, sblock, tile_rows), pair_map, axis=0)
    result = jnp.einsum("psa,psc->ac", block_coeffs, incoming, preferred_element_type=jnp.float32)
    return result.reshape(tile_rows, local_j, num_virt)


LANES = 128


def kernel(
    num_pair, num_i, local_tiles,
    pm_ref, tt_ref, h_ref, c_ref, o_ref,
    hs, hr, c_all, ct, tiles, ts, tr,
    c_send, c_recv, f_send, f_recv, p_send, p_recv, h_send, h_recv, t_send, t_recv,
):
    me = lax.axis_index("pair")
    occ = lax.axis_index("occ")
    sblock, num_virt = c_ref.shape[1], c_ref.shape[2]
    per = c_ref.shape[0]
    tile_rows = num_virt // local_tiles
    half = num_virt // 2
    partner = occ + 1 - 2 * lax.rem(occ, 2)
    cross = lax.rem(occ + 2, 4)
    diagonal = cross + 1 - 2 * lax.rem(cross, 2)
    peers = [{"pair": lax.rem(me + d, num_pair)} for d in range(1, num_pair)]
    peers += [{"occ": partner}, {"occ": cross}]
    barrier = pltpu.get_barrier_semaphore()
    for peer in peers:
        pl.semaphore_signal(barrier, inc=1, device_id=peer, device_id_type=pl.DeviceIdType.MESH)

    def remote(source, target, send, recv, where):
        return pltpu.make_async_remote_copy(
            src_ref=source, dst_ref=target, send_sem=send, recv_sem=recv,
            device_id=where, device_id_type=pl.DeviceIdType.MESH,
        )

    pad = jnp.zeros((sblock, LANES - sblock), jnp.bfloat16)
    for p in range(num_pair):
        for i in range(num_i):
            piece = h_ref[i, :, p * sblock:(p + 1) * sblock]
            hs[p, :, i * LANES:(i + 1) * LANES] = jnp.concatenate([piece, pad], axis=1)

    pl.semaphore_wait(barrier, len(peers))

    chunks = [(h, b) for h in range(2) for b in range(per)]
    to_cross, relay, from_relay = [], [], []
    for q, (h, b) in enumerate(chunks):
        cols = pl.ds(h * half, half)
        to_cross.append(remote(
            c_ref.at[b, :, cols], c_all.at[per * occ + b, :, cols],
            c_send.at[q], c_recv.at[q], {"occ": cross}))
        spot = c_all.at[per * cross + b, :, cols]
        relay.append(remote(spot, spot, f_send.at[q], f_recv.at[q], {"occ": partner}))
    to_partner = remote(
        c_ref, c_all.at[pl.ds(per * occ, per)], p_send, p_recv, {"occ": partner})
    for copy in to_cross:
        copy.start()
    to_partner.start()
    h_copies = []
    for d in range(1, num_pair):
        dest = lax.rem(me + d, num_pair)
        h_copies.append(remote(
            hs.at[dest], hr.at[d], h_send.at[d], h_recv.at[d], {"pair": dest}))
    for copy in h_copies:
        copy.start()

    def turn(owner, b, h):
        block = c_all[per * owner + b, :, h * half:(h + 1) * half]
        ct[per * owner + b, h * half:(h + 1) * half, :] = block.T

    for b in range(per):
        c_all[per * occ + b] = c_ref[b]
    for h, b in chunks:
        turn(occ, b, h)
    to_partner.wait_recv()
    for h, b in chunks:
        turn(partner, b, h)
    for q, (h, b) in enumerate(chunks):
        to_cross[q].wait_recv()
        relay[q].start()
        turn(cross, b, h)
    for q, (h, b) in enumerate(chunks):
        relay[q].wait_recv()
        turn(diagonal, b, h)
    for copy in h_copies:
        copy.wait_recv()

    for j in range(local_tiles):
        rows = slice(j * tile_rows, (j + 1) * tile_rows)
        total = jnp.zeros((tile_rows, num_i * LANES), jnp.float32)
        for d in range(num_pair):
            src = lax.rem(me + num_pair - d, num_pair)
            block = hs[me] if d == 0 else hr[d]
            total += jnp.dot(ct[pm_ref[src], rows, :], block, preferred_element_type=jnp.float32)
        total = total.astype(jnp.bfloat16)
        for i in range(num_i):
            tiles[i * local_tiles + j] = total[:, i * LANES:i * LANES + sblock]

    t_copies = []
    for d in range(1, num_pair):
        dest = lax.rem(me + d, num_pair)
        ts[d] = tiles[tt_ref[dest]]
        copy = remote(ts.at[d], tr.at[d], t_send.at[d], t_recv.at[d], {"pair": dest})
        copy.start()
        t_copies.append(copy)
    tr[0] = tiles[tt_ref[me]]
    for copy in t_copies:
        copy.wait_recv()
    wide = 2 * LANES
    per_row = num_virt // LANES
    for n in range(num_virt // wide):
        total = jnp.zeros((tile_rows, wide), jnp.float32)
        for d in range(num_pair):
            src = lax.rem(me + num_pair - d, num_pair)
            total += jnp.dot(
                tr[d], c_all[src, :, n * wide:(n + 1) * wide], preferred_element_type=jnp.float32)
        for m in range(2):
            o_ref[pl.ds(2 * n + m, tile_rows, stride=per_row), :] = total[:, m * LANES:(m + 1) * LANES]

    for copy in to_cross + relay + [to_partner] + h_copies + t_copies:
        copy.wait_send()


def shards_kernel(half_ints, coeffs, pair_map, tile_table):
    num_i, sblock, local_j, num_basis = half_ints.shape
    num_virt = coeffs.shape[1]
    num_pair = lax.axis_size("pair")
    local_tiles = num_pair // num_i
    tile_rows = num_virt // local_tiles
    per = coeffs.shape[0] // sblock
    ints = half_ints.reshape(num_i, sblock, num_basis)
    mine = coeffs.reshape(per, sblock, num_virt)
    bf16 = jnp.bfloat16
    dma = pltpu.SemaphoreType.DMA
    vmem = pl.BlockSpec(memory_space=pltpu.VMEM)
    smem = pl.BlockSpec(memory_space=pltpu.SMEM)
    out = pl.pallas_call(
        functools.partial(kernel, num_pair, num_i, local_tiles),
        out_shape=jax.ShapeDtypeStruct((tile_rows * num_virt // LANES, LANES), jnp.float32),
        in_specs=[smem, smem, vmem, vmem],
        out_specs=vmem,
        scratch_shapes=[
            pltpu.VMEM((num_pair, sblock, num_i * LANES), bf16),
            pltpu.VMEM((num_pair, sblock, num_i * LANES), bf16),
            pltpu.VMEM((num_pair, sblock, num_virt), bf16),
            pltpu.VMEM((num_pair, num_virt, sblock), bf16),
            pltpu.VMEM((num_pair, tile_rows, sblock), bf16),
            pltpu.VMEM((num_pair, tile_rows, sblock), bf16),
            pltpu.VMEM((num_pair, tile_rows, sblock), bf16),
            dma((2 * per,)), dma((2 * per,)), dma((2 * per,)), dma((2 * per,)),
            dma, dma,
            dma((num_pair,)), dma((num_pair,)), dma((num_pair,)), dma((num_pair,)),
        ],
        compiler_params=pltpu.CompilerParams(
            collective_id=0, has_side_effects=True, vmem_limit_bytes=40 * 1024 * 1024),
    )(pair_map, tile_table, ints, mine)
    return out.reshape(tile_rows, local_j, num_virt)


def shards(half_ints, coeffs, pair_map, tile_table):
    num_i, sblock, local_j, num_basis = half_ints.shape
    num_virt = coeffs.shape[1]
    num_pair = lax.axis_size("pair")
    fits = (
        num_i == 2 and local_j == 1 and lax.axis_size("occ") == 4
        and sblock % 16 == 0 and sblock < LANES and sblock * num_pair == num_basis
        and num_pair % 4 == 0 and num_virt % (2 * LANES) == 0
        and num_virt % (16 * (num_pair // num_i)) == 0
    )
    body = shards_kernel if fits else shards_general
    return body(half_ints, coeffs, pair_map, tile_table)


def solution(mesh):
    placed = (P(None, "pair", "occ", None), P("occ", None), P(), P())
    return jax.shard_map(
        shards, mesh=mesh, in_specs=placed, out_specs=P("pair", "occ", None), check_vma=False
    )
```

```python
import functools

import jax
import jax.numpy as jnp
from jax import lax
from jax.experimental import pallas as pl
from jax.experimental.pallas import tpu as pltpu
from jax.sharding import PartitionSpec as P


def shards_general(half_ints, coeffs, pair_map, tile_table):
    num_occ = half_ints.shape[0]
    sblock = half_ints.shape[1]
    local_j = half_ints.shape[2]
    num_basis = half_ints.shape[3]
    num_virt = coeffs.shape[1]
    num_pair = lax.axis_size("pair")
    tile_rows = num_occ * num_virt // num_pair
    all_coeffs = lax.all_gather(coeffs, "occ", axis=0, tiled=True)
    flat_ints = half_ints.reshape(num_occ * sblock * local_j, num_basis)
    half_mo = jnp.dot(flat_ints, all_coeffs, preferred_element_type=jnp.float32).astype(
        jnp.bfloat16
    )
    half_mo = half_mo.reshape(num_occ, sblock, local_j, num_virt)
    tile_id = tile_table[lax.axis_index("pair")]
    virt_start = tile_id * tile_rows % num_virt
    column_coeffs = lax.dynamic_slice_in_dim(all_coeffs, virt_start, tile_rows, 1)
    half_flat = half_mo.reshape(num_occ, sblock, local_j * num_virt)
    slot_occ = tile_table * tile_rows // num_virt
    outgoing = jnp.take(half_flat, slot_occ, axis=0)
    incoming = lax.all_to_all(outgoing, "pair", split_axis=0, concat_axis=0, tiled=True)
    block_coeffs = jnp.take(column_coeffs.reshape(num_pair, sblock, tile_rows), pair_map, axis=0)
    result = jnp.einsum("psa,psc->ac", block_coeffs, incoming, preferred_element_type=jnp.float32)
    return result.reshape(tile_rows, local_j, num_virt)


LANES = 128


def kernel(
    num_pair, num_i, local_tiles,
    pm_hbm, tt_hbm, h_hbm, c_ref, o_ref,
    pm_ref, tt_ref, h_ref, in_sem, hs, hr, c_all, ct, half_sum, tiles, ts, tr, out_sum,
    c_send, c_recv, f_send, f_recv, p_send, p_recv, h_send, h_recv, t_send, t_recv, ring_sem, side_sem,
):
    me = lax.axis_index("pair")
    occ = lax.axis_index("occ")
    ring = num_pair // 2
    z, y = me // 2, lax.rem(me, 2)
    sblock, num_virt = c_ref.shape[1], c_ref.shape[2]
    per = c_ref.shape[0]
    tile_rows = num_virt // local_tiles
    half = num_virt // 2
    partner = occ + 1 - 2 * lax.rem(occ, 2)
    cross = lax.rem(occ + 2, 4)
    diagonal = cross + 1 - 2 * lax.rem(cross, 2)
    MESH = pl.DeviceIdType.MESH

    def ahead(k):
        return 2 * lax.rem(z + k // 2, ring) + lax.rem(y + k, 2)

    def behind(k):
        return 2 * lax.rem(z + ring - k // 2, ring) + lax.rem(y + k, 2)

    near = (1, 2, 2 * ring - 2)
    groups = ((0, 1, 2, 6), (3, 7, 4), (5,))
    send_order = (5, 4, 3, 7, 2, 6, 1)

    fetch_c = pltpu.make_async_copy(c_ref, c_all.at[pl.ds(per * occ, per)], in_sem.at[1])
    fetch_h = pltpu.make_async_copy(h_hbm, h_ref, in_sem.at[0])
    fetch_pm = pltpu.make_async_copy(pm_hbm, pm_ref, in_sem.at[2])
    fetch_tt = pltpu.make_async_copy(tt_hbm, tt_ref, in_sem.at[3])
    barrier = pltpu.get_barrier_semaphore()
    greeted = [{"occ": partner}, {"occ": cross}] + [{"pair": ahead(k)} for k in range(1, num_pair)]
    for peer in greeted:
        pl.semaphore_signal(barrier, inc=1, device_id=peer, device_id_type=MESH)
    for fetch in (fetch_h, fetch_c, fetch_pm, fetch_tt):
        fetch.start()

    def remote(source, target, send, recv, where):
        return pltpu.make_async_remote_copy(
            src_ref=source, dst_ref=target, send_sem=send, recv_sem=recv,
            device_id=where, device_id_type=MESH,
        )

    chunks = [(h, b) for h in range(2) for b in range(per)]
    to_cross, relay = [], []
    for q, (h, b) in enumerate(chunks):
        cols = pl.ds(h * half, half)
        to_cross.append(remote(
            c_ref.at[b, :, cols], c_all.at[per * occ + b, :, cols],
            c_send.at[q], c_recv.at[q], {"occ": cross}))
        spot = c_all.at[per * cross + b, :, cols]
        relay.append(remote(spot, spot, f_send.at[q], f_recv.at[q], {"occ": partner}))
    to_partner = remote(
        c_ref, c_all.at[pl.ds(per * occ, per)], p_send, p_recv, {"occ": partner})
    h_copies = {
        k: remote(hs.at[ahead(k)], hr.at[k], h_send.at[k], h_recv.at[k], {"pair": ahead(k)})
        for k in range(1, num_pair)}
    t_copies = {
        k: remote(ts.at[k], tr.at[k], t_send.at[k], t_recv.at[k], {"pair": ahead(k)})
        for k in range(1, num_pair)}

    fetch_h.wait()
    pad = jnp.zeros((sblock, LANES - sblock), jnp.bfloat16)
    for p in range(num_pair):
        for i in range(num_i):
            piece = h_ref[i, :, p * sblock:(p + 1) * sblock]
            hs[p, :, i * LANES:(i + 1) * LANES] = jnp.concatenate([piece, pad], axis=1)

    pl.semaphore_wait(barrier, len(greeted))
    for copy in to_cross:
        copy.start()
    to_partner.start()

    early = ()
    for k in early:
        h_copies[k].start()
    for n in range(1, num_pair):
        k = (0, 1, 2, 3, 4, 5, 6, 7)[n] + y * ((0, 3, 2, 5, 4, 7, 6, 1)[n] - (0, 1, 2, 3, 4, 5, 6, 7)[n])
        remote(hs.at[ahead(k)], hr.at[k], h_send.at[k], h_recv.at[k], {"pair": ahead(k)}).start()

    def turn(owner, b, h):
        block = c_all[per * owner + b, :, h * half:(h + 1) * half]
        ct[per * owner + b, h * half:(h + 1) * half, :] = block.T

    for fetch in (fetch_c, fetch_pm, fetch_tt):
        fetch.wait()
    for h, b in chunks:
        turn(occ, b, h)
    to_partner.wait_recv()
    for h, b in chunks:
        turn(partner, b, h)
    for q, (h, b) in enumerate(chunks):
        to_cross[q].wait_recv()
        relay[q].start()
        turn(cross, b, h)
    for q, (h, b) in enumerate(chunks):
        relay[q].wait_recv()
        turn(diagonal, b, h)

    last = len(groups) - 1
    for g, group in enumerate(groups):
        for k in group:
            if k > 0:
                h_copies[k].wait_recv()
        for j in range(local_tiles):
            rows = slice(j * tile_rows, (j + 1) * tile_rows)
            total = half_sum[rows, :] if g > 0 else None
            for k in group:
                block = hs[me] if k == 0 else hr[k]
                term = jnp.dot(
                    ct[pm_ref[behind(k)], rows, :], block, preferred_element_type=jnp.float32)
                total = term if total is None else total + term
            if g < last:
                half_sum[rows, :] = total
            else:
                total = total.astype(jnp.bfloat16)
                for i in range(num_i):
                    tiles[i * local_tiles + j] = total[:, i * LANES:i * LANES + sblock]

    for n in range(1, num_pair):
        k = (0, 1, 2, 3, 4, 5, 6, 7)[n] + y * ((0, 3, 2, 5, 4, 7, 6, 1)[n] - (0, 1, 2, 3, 4, 5, 6, 7)[n])
        ts[k] = tiles[tt_ref[ahead(k)]]
        remote(ts.at[k], tr.at[k], t_send.at[k], t_recv.at[k], {"pair": ahead(k)}).start()
    tr[0] = tiles[tt_ref[me]]
    wide = 2 * LANES
    per_row = num_virt // LANES
    for g, group in enumerate(groups):
        for k in group:
            if k > 0:
                t_copies[k].wait_recv()
        for n in range(num_virt // wide):
            cols = slice(n * wide, (n + 1) * wide)
            total = out_sum[:, cols] if g > 0 else None
            for k in group:
                term = jnp.dot(
                    tr[k], c_all[behind(k), :, cols], preferred_element_type=jnp.float32)
                total = term if total is None else total + term
            if g < last:
                out_sum[:, cols] = total
            else:
                for m in range(2):
                    o_ref[pl.ds(2 * n + m, tile_rows, stride=per_row), :] = (
                        total[:, m * LANES:(m + 1) * LANES])

    for copy in to_cross + relay + [to_partner] + list(h_copies.values()) + list(t_copies.values()):
        copy.wait_send()


def shards_kernel(half_ints, coeffs, pair_map, tile_table):
    num_i, sblock, local_j, num_basis = half_ints.shape
    num_virt = coeffs.shape[1]
    num_pair = lax.axis_size("pair")
    local_tiles = num_pair // num_i
    tile_rows = num_virt // local_tiles
    per = coeffs.shape[0] // sblock
    ints = half_ints.reshape(num_i, sblock, num_basis)
    mine = coeffs.reshape(per, sblock, num_virt)
    bf16 = jnp.bfloat16
    dma = pltpu.SemaphoreType.DMA
    vmem = pl.BlockSpec(memory_space=pltpu.VMEM)
    hbm = pl.BlockSpec(memory_space=pltpu.HBM)
    ints, mine, pair_map, tile_table = (
        pltpu.with_memory_space_constraint(a, pltpu.HBM) for a in (ints, mine, pair_map, tile_table))
    out = pl.pallas_call(
        functools.partial(kernel, num_pair, num_i, local_tiles),
        out_shape=jax.ShapeDtypeStruct((tile_rows * num_virt // LANES, LANES), jnp.float32),
        in_specs=[hbm, hbm, hbm, hbm],
        out_specs=vmem,
        scratch_shapes=[
            pltpu.SMEM(pair_map.shape, jnp.int32),
            pltpu.SMEM(tile_table.shape, jnp.int32),
            pltpu.VMEM(ints.shape, bf16),
            dma((4,)),
            pltpu.VMEM((num_pair, sblock, num_i * LANES), bf16),
            pltpu.VMEM((num_pair, sblock, num_i * LANES), bf16),
            pltpu.VMEM((num_pair, sblock, num_virt), bf16),
            pltpu.VMEM((num_pair, num_virt, sblock), bf16),
            pltpu.VMEM((num_virt, num_i * LANES), jnp.float32),
            pltpu.VMEM((num_pair, tile_rows, sblock), bf16),
            pltpu.VMEM((num_pair, tile_rows, sblock), bf16),
            pltpu.VMEM((num_pair, tile_rows, sblock), bf16),
            pltpu.VMEM((tile_rows, num_virt), jnp.float32),
            dma((2 * per,)), dma((2 * per,)), dma((2 * per,)), dma((2 * per,)),
            dma, dma,
            dma((num_pair,)), dma((num_pair,)), dma((num_pair,)), dma((num_pair,)),
            pltpu.SemaphoreType.REGULAR, pltpu.SemaphoreType.REGULAR,
        ],
        compiler_params=pltpu.CompilerParams(
            collective_id=0, has_side_effects=True, vmem_limit_bytes=40 * 1024 * 1024),
    )(pair_map, tile_table, ints, mine)
    return out.reshape(tile_rows, local_j, num_virt)


def shards(half_ints, coeffs, pair_map, tile_table):
    num_i, sblock, local_j, num_basis = half_ints.shape
    num_virt = coeffs.shape[1]
    num_pair = lax.axis_size("pair")
    fits = (
        num_i == 2 and local_j == 1 and lax.axis_size("occ") == 4
        and sblock % 16 == 0 and sblock < LANES and sblock * num_pair == num_basis
        and num_pair == 8 and num_virt % (2 * LANES) == 0
        and num_virt % (16 * (num_pair // num_i)) == 0
    )
    body = shards_kernel if fits else shards_general
    return body(half_ints, coeffs, pair_map, tile_table)


def solution(mesh):
    placed = (P(None, "pair", "occ", None), P("occ", None), P(), P())
    return jax.shard_map(
        shards, mesh=mesh, in_specs=placed, out_specs=P("pair", "occ", None), check_vma=False
    )
```

```python
import functools

import jax
import jax.numpy as jnp
from jax import lax
from jax.experimental import pallas as pl
from jax.experimental.pallas import tpu as pltpu
from jax.sharding import PartitionSpec as P


def shards_general(half_ints, coeffs, pair_map, tile_table):
    num_occ = half_ints.shape[0]
    sblock = half_ints.shape[1]
    local_j = half_ints.shape[2]
    num_basis = half_ints.shape[3]
    num_virt = coeffs.shape[1]
    num_pair = lax.axis_size("pair")
    tile_rows = num_occ * num_virt // num_pair
    all_coeffs = lax.all_gather(coeffs, "occ", axis=0, tiled=True)
    flat_ints = half_ints.reshape(num_occ * sblock * local_j, num_basis)
    half_mo = jnp.dot(flat_ints, all_coeffs, preferred_element_type=jnp.float32).astype(
        jnp.bfloat16
    )
    half_mo = half_mo.reshape(num_occ, sblock, local_j, num_virt)
    tile_id = tile_table[lax.axis_index("pair")]
    virt_start = tile_id * tile_rows % num_virt
    column_coeffs = lax.dynamic_slice_in_dim(all_coeffs, virt_start, tile_rows, 1)
    half_flat = half_mo.reshape(num_occ, sblock, local_j * num_virt)
    slot_occ = tile_table * tile_rows // num_virt
    outgoing = jnp.take(half_flat, slot_occ, axis=0)
    incoming = lax.all_to_all(outgoing, "pair", split_axis=0, concat_axis=0, tiled=True)
    block_coeffs = jnp.take(column_coeffs.reshape(num_pair, sblock, tile_rows), pair_map, axis=0)
    result = jnp.einsum("psa,psc->ac", block_coeffs, incoming, preferred_element_type=jnp.float32)
    return result.reshape(tile_rows, local_j, num_virt)


LANES = 128


def kernel(
    num_pair, num_i, local_tiles,
    pm_hbm, tt_hbm, h_hbm, c_ref, o_ref,
    pm_ref, tt_ref, h_ref, in_sem, hs, hr, c_all, ct, half_sum, tiles, ts, tr, out_sum,
    c_send, c_recv, f_send, f_recv, p_send, p_recv, h_send, h_recv, t_send, t_recv,
):
    me = lax.axis_index("pair")
    occ = lax.axis_index("occ")
    ring = num_pair // 2
    z, y = me // 2, lax.rem(me, 2)
    sblock, num_virt = c_ref.shape[1], c_ref.shape[2]
    per = c_ref.shape[0]
    tile_rows = num_virt // local_tiles
    half = num_virt
    partner = occ + 1 - 2 * lax.rem(occ, 2)
    cross = lax.rem(occ + 2, 4)
    diagonal = cross + 1 - 2 * lax.rem(cross, 2)
    MESH = pl.DeviceIdType.MESH

    def ahead(k):
        return 2 * lax.rem(z + k // 2, ring) + lax.rem(y + k, 2)

    def behind(k):
        return 2 * lax.rem(z + ring - k // 2, ring) + lax.rem(y + k, 2)

    groups = ((0, 1, 2, 6), (3, 7, 4), (5,))

    fetch_c = pltpu.make_async_copy(c_ref, c_all.at[pl.ds(per * occ, per)], in_sem.at[1])
    fetch_h = pltpu.make_async_copy(h_hbm, h_ref, in_sem.at[0])
    fetch_pm = pltpu.make_async_copy(pm_hbm, pm_ref, in_sem.at[2])
    fetch_tt = pltpu.make_async_copy(tt_hbm, tt_ref, in_sem.at[3])
    barrier = pltpu.get_barrier_semaphore()
    greeted = [{"occ": partner}, {"occ": cross}] + [{"pair": ahead(k)} for k in range(1, num_pair)]
    for peer in greeted:
        pl.semaphore_signal(barrier, inc=1, device_id=peer, device_id_type=MESH)
    for fetch in (fetch_h, fetch_c, fetch_pm, fetch_tt):
        fetch.start()

    def remote(source, target, send, recv, where):
        return pltpu.make_async_remote_copy(
            src_ref=source, dst_ref=target, send_sem=send, recv_sem=recv,
            device_id=where, device_id_type=MESH,
        )

    chunks = [(h, b) for h in range(1) for b in range(per)]
    to_cross, relay = [], []
    for q, (h, b) in enumerate(chunks):
        cols = pl.ds(h * half, half)
        to_cross.append(remote(
            c_all.at[per * occ + b, :, cols], c_all.at[per * occ + b, :, cols],
            c_send.at[q], c_recv.at[q], {"occ": cross}))
        spot = c_all.at[per * cross + b, :, cols]
        relay.append(remote(spot, spot, f_send.at[q], f_recv.at[q], {"occ": partner}))
    to_partner = remote(
        c_all.at[pl.ds(per * occ, per)], c_all.at[pl.ds(per * occ, per)], p_send, p_recv, {"occ": partner})
    h_copies = {
        k: remote(hs.at[ahead(k)], hr.at[k], h_send.at[k], h_recv.at[k], {"pair": ahead(k)})
        for k in range(1, num_pair)}
    t_copies = {
        k: remote(ts.at[k], tr.at[k], t_send.at[k], t_recv.at[k], {"pair": ahead(k)})
        for k in range(1, num_pair)}

    fetch_h.wait()
    pad = jnp.zeros((sblock, LANES - sblock), jnp.bfloat16)
    for p in range(num_pair):
        for i in range(num_i):
            piece = h_ref[i, :, p * sblock:(p + 1) * sblock]
            hs[p, :, i * LANES:(i + 1) * LANES] = jnp.concatenate([piece, pad], axis=1)

    fetch_c.wait()
    pl.semaphore_wait(barrier, len(greeted))
    for copy in to_cross:
        copy.start()
    to_partner.start()


    for n in range(1, num_pair):
        k = (0, 1, 2, 3, 4, 5, 6, 7)[n] + y * ((0, 3, 2, 5, 4, 7, 6, 1)[n] - (0, 1, 2, 3, 4, 5, 6, 7)[n])
        remote(hs.at[ahead(k)], hr.at[k], h_send.at[k], h_recv.at[k], {"pair": ahead(k)}).start()

    def turn(owner, b, h):
        block = c_all[per * owner + b, :, h * half:(h + 1) * half]
        ct[per * owner + b, h * half:(h + 1) * half, :] = block.T

    for fetch in (fetch_pm, fetch_tt):
        fetch.wait()
    for h, b in chunks:
        turn(occ, b, h)
    to_partner.wait_recv()
    for h, b in chunks:
        turn(partner, b, h)
    for q, (h, b) in enumerate(chunks):
        to_cross[q].wait_recv()
        relay[q].start()
        turn(cross, b, h)
    for q, (h, b) in enumerate(chunks):
        relay[q].wait_recv()
        turn(diagonal, b, h)

    last = len(groups) - 1
    for g, group in enumerate(groups):
        for k in group:
            if k > 0:
                h_copies[k].wait_recv()
        for j in range(local_tiles):
            rows = slice(j * tile_rows, (j + 1) * tile_rows)
            total = half_sum[rows, :] if g > 0 else None
            for k in group:
                block = hs[me] if k == 0 else hr[k]
                term = jnp.dot(
                    ct[pm_ref[behind(k)], rows, :], block, preferred_element_type=jnp.float32)
                total = term if total is None else total + term
            if g < last:
                half_sum[rows, :] = total
            else:
                total = total.astype(jnp.bfloat16)
                for i in range(num_i):
                    tiles[i * local_tiles + j] = total[:, i * LANES:i * LANES + sblock]

    for n in range(1, num_pair):
        k = (0, 1, 2, 3, 4, 5, 6, 7)[n] + y * ((0, 3, 2, 5, 4, 7, 6, 1)[n] - (0, 1, 2, 3, 4, 5, 6, 7)[n])
        ts[k] = tiles[tt_ref[ahead(k)]]
        remote(ts.at[k], tr.at[k], t_send.at[k], t_recv.at[k], {"pair": ahead(k)}).start()
    tr[0] = tiles[tt_ref[me]]
    wide = 2 * LANES
    per_row = num_virt // LANES
    for g, group in enumerate(groups):
        for k in group:
            if k > 0:
                t_copies[k].wait_recv()
        for n in range(num_virt // wide):
            cols = slice(n * wide, (n + 1) * wide)
            total = out_sum[:, cols] if g > 0 else None
            for k in group:
                term = jnp.dot(
                    tr[k], c_all[behind(k), :, cols], preferred_element_type=jnp.float32)
                total = term if total is None else total + term
            if g < last:
                out_sum[:, cols] = total
            else:
                for m in range(2):
                    o_ref[pl.ds(2 * n + m, tile_rows, stride=per_row), :] = (
                        total[:, m * LANES:(m + 1) * LANES])

    for copy in to_cross + relay + [to_partner] + list(h_copies.values()) + list(t_copies.values()):
        copy.wait_send()


def shards_kernel(half_ints, coeffs, pair_map, tile_table):
    num_i, sblock, local_j, num_basis = half_ints.shape
    num_virt = coeffs.shape[1]
    num_pair = lax.axis_size("pair")
    local_tiles = num_pair // num_i
    tile_rows = num_virt // local_tiles
    per = coeffs.shape[0] // sblock
    ints = half_ints.reshape(num_i, sblock, num_basis)
    mine = coeffs.reshape(per, sblock, num_virt)
    bf16 = jnp.bfloat16
    dma = pltpu.SemaphoreType.DMA
    vmem = pl.BlockSpec(memory_space=pltpu.VMEM)
    hbm = pl.BlockSpec(memory_space=pltpu.HBM)
    ints, mine, pair_map, tile_table = (
        pltpu.with_memory_space_constraint(a, pltpu.HBM) for a in (ints, mine, pair_map, tile_table))
    out = pl.pallas_call(
        functools.partial(kernel, num_pair, num_i, local_tiles),
        out_shape=jax.ShapeDtypeStruct((tile_rows * num_virt // LANES, LANES), jnp.float32),
        in_specs=[hbm, hbm, hbm, hbm],
        out_specs=vmem,
        scratch_shapes=[
            pltpu.SMEM(pair_map.shape, jnp.int32),
            pltpu.SMEM(tile_table.shape, jnp.int32),
            pltpu.VMEM(ints.shape, bf16),
            dma((4,)),
            pltpu.VMEM((num_pair, sblock, num_i * LANES), bf16),
            pltpu.VMEM((num_pair, sblock, num_i * LANES), bf16),
            pltpu.VMEM((num_pair, sblock, num_virt), bf16),
            pltpu.VMEM((num_pair, num_virt, sblock), bf16),
            pltpu.VMEM((num_virt, num_i * LANES), jnp.float32),
            pltpu.VMEM((num_pair, tile_rows, sblock), bf16),
            pltpu.VMEM((num_pair, tile_rows, sblock), bf16),
            pltpu.VMEM((num_pair, tile_rows, sblock), bf16),
            pltpu.VMEM((tile_rows, num_virt), jnp.float32),
            dma((2 * per,)), dma((2 * per,)), dma((2 * per,)), dma((2 * per,)),
            dma, dma,
            dma((num_pair,)), dma((num_pair,)), dma((num_pair,)), dma((num_pair,)),
        ],
        compiler_params=pltpu.CompilerParams(
            collective_id=0, has_side_effects=True, vmem_limit_bytes=40 * 1024 * 1024),
    )(pair_map, tile_table, ints, mine)
    return out.reshape(tile_rows, local_j, num_virt)


def shards(half_ints, coeffs, pair_map, tile_table):
    num_i, sblock, local_j, num_basis = half_ints.shape
    num_virt = coeffs.shape[1]
    num_pair = lax.axis_size("pair")
    fits = (
        num_i == 2 and local_j == 1 and lax.axis_size("occ") == 4
        and sblock % 16 == 0 and sblock < LANES and sblock * num_pair == num_basis
        and num_pair == 8 and num_virt % (2 * LANES) == 0
        and num_virt % (16 * (num_pair // num_i)) == 0
    )
    body = shards_kernel if fits else shards_general
    return body(half_ints, coeffs, pair_map, tile_table)


def solution(mesh):
    placed = (P(None, "pair", "occ", None), P("occ", None), P(), P())
    return jax.shard_map(
        shards, mesh=mesh, in_specs=placed, out_specs=P("pair", "occ", None), check_vma=False
    )
```
